32 devices in a mesh: dp: 4 (over y, x), rows: 2 (over core), tm: 4 (over z).
Axes of the slice: x: 2, y: 2, z: 4, core: 2. Of those that a mesh axis runs over, the one named last changes fastest.
Arguments:
- video_cells: bfloat16 [4, 8, 8, 128, 128], P('dp', 'tm', 'rows'), may hold values from -6 to 6
- block_weight: bfloat16 [3, 3, 3, 128, 128], replicated, may hold values from -0.109375 to 0.109375
- down_weight: bfloat16 [3, 3, 3, 128, 256], replicated, may hold values from -0.109375 to 0.109375
- cotangent: bfloat16 [4, 4, 4, 64, 256], P('dp', 'tm', 'rows'), may hold values from -6 to 6
Outputs:
- latents: bfloat16 [4, 4, 4, 64, 256], P('dp', 'tm', 'rows')
- grad_video: bfloat16 [4, 8, 8, 128, 128], P('dp', 'tm', 'rows')
- grad_block: float32 [3, 3, 3, 128, 128], replicated
- grad_down: float32 [3, 3, 3, 128, 256], replicated
The draws below stay inside these ranges and needn't reach their ends.
All inputs are finite; a program needn't handle non-finite values.
Results may differ from the reference program's by a relative error of at most 0.0055.
Values may be sent and summed in bfloat16 or wider, within the bound.
A program may use at most 64 MiB of HBM per device.

```python
import jax
import jax.numpy as jnp

C = 128
C2 = 256
W = 128
CLIPS = 4
FRAMES = 8
HEIGHT = 8


def block_levels(stream_key, shape, shards, low, largest):
    loudness, own = 1.0, jax.random.fold_in(stream_key, 6)
    for dim, blocks in shards:
        draws = jnp.exp(jax.random.uniform(jax.random.fold_in(own, dim), (blocks,), jnp.float32, low / len(shards), largest / len(shards)))
        loudness = loudness * jnp.repeat(draws, shape[dim] // blocks).reshape([-1 if axis == dim else 1 for axis in range(len(shape))])
    return loudness


def scatter_about(rng, extent, width, reach, shards=(), dtype=jnp.bfloat16):
    values = jax.random.normal(rng, extent, jnp.float32) * width
    if len(shards) > 0:
        values = block_levels(rng, extent, shards, -0.22, 0.18) * values
    return jnp.clip(values, min=-reach, max=reach).astype(dtype)


def setup_inputs(seed: int = 0) -> dict:
    key_list = jax.random.split(jax.random.key(seed), 5)
    video_cells = scatter_about(key_list[0], (CLIPS, FRAMES, HEIGHT, W, C), 1.0, 6.0, ((0, 4), (1, 4), (2, 2)))
    block_weight = scatter_about(key_list[1], (3, 3, 3, C, C), (27 * C) ** -0.5, 0.109375)
    down_weight = scatter_about(key_list[2], (3, 3, 3, C, C2), (27 * C) ** -0.5, 0.109375)
    cotangent = scatter_about(key_list[3], (CLIPS, FRAMES // 2, HEIGHT // 2, W // 2, C2), 1.0, 6.0, ((0, 4), (1, 4), (2, 2)))
    return {"video_cells": video_cells, "block_weight": block_weight, "down_weight": down_weight, "cotangent": cotangent}


def tap_list():
    return [(frame_tap, row_tap, column_tap) for frame_tap in range(3) for row_tap in range(3) for column_tap in range(3)]


def flat_dot(operand, matrix):
    result = jnp.dot(operand.reshape(-1, operand.shape[-1]), matrix, preferred_element_type=jnp.float32)
    return result.reshape(operand.shape[:-1] + (matrix.shape[-1],))


def outer_sum(operand, cotangent_part):
    return jnp.dot(operand.reshape(-1, operand.shape[-1]).T, cotangent_part.reshape(-1, cotangent_part.shape[-1]), preferred_element_type=jnp.float32)


def reference(video_cells, block_weight, down_weight, cotangent):
    clip_count, frames, height, columns, channels = video_cells.shape
    wide_channels = down_weight.shape[-1]
    source = video_cells.astype(jnp.float32)
    activated = jax.nn.silu(source).astype(jnp.bfloat16)
    padded_a = jnp.pad(activated, ((0, 0), (2, 0), (1, 1), (1, 1), (0, 0)))
    branch = jnp.zeros(source.shape, jnp.float32)
    for frame_tap, row_tap, column_tap in tap_list():
        window = padded_a[:, frame_tap:frame_tap + frames, row_tap:row_tap + height, column_tap:column_tap + columns]
        branch = branch + flat_dot(window, block_weight[frame_tap, row_tap, column_tap])
    summed = (source + branch).astype(jnp.bfloat16)
    padded_b = jnp.pad(summed, ((0, 0), (1, 0), (1, 0), (1, 0), (0, 0)))
    latents = jnp.zeros((clip_count, frames // 2, height // 2, columns // 2, wide_channels), jnp.float32)
    buffer = jnp.zeros((clip_count, frames + 1, height + 1, columns + 1, channels), jnp.float32)
    down_terms = []
    for frame_tap, row_tap, column_tap in tap_list():
        window = padded_b[:, frame_tap:frame_tap + frames - 1:2, row_tap:row_tap + height - 1:2, column_tap:column_tap + columns - 1:2]
        kernel = down_weight[frame_tap, row_tap, column_tap]
        latents = latents + flat_dot(window, kernel)
        buffer = buffer.at[:, frame_tap:frame_tap + frames - 1:2, row_tap:row_tap + height - 1:2, column_tap:column_tap + columns - 1:2].add(flat_dot(cotangent, kernel.T))
        down_terms.append(outer_sum(window, cotangent))
    grad_summed = buffer[:, 1:, 1:, 1:].astype(jnp.bfloat16)
    padded_g = jnp.pad(grad_summed, ((0, 0), (0, 2), (1, 1), (1, 1), (0, 0)))
    grad_activated = jnp.zeros(source.shape, jnp.float32)
    block_terms = []
    for frame_tap, row_tap, column_tap in tap_list():
        window = padded_g[:, 2 - frame_tap:2 - frame_tap + frames, 2 - row_tap:2 - row_tap + height, 2 - column_tap:2 - column_tap + columns]
        grad_activated = grad_activated + flat_dot(window, block_weight[frame_tap, row_tap, column_tap].T)
        forward_window = padded_a[:, frame_tap:frame_tap + frames, row_tap:row_tap + height, column_tap:column_tap + columns]
        block_terms.append(outer_sum(forward_window, grad_summed))
    sigmoid_value = jax.nn.sigmoid(source)
    grad_video = (grad_summed.astype(jnp.float32) + grad_activated * sigmoid_value * (1.0 + source * (1.0 - sigmoid_value))).astype(jnp.bfloat16)
    total_cells = clip_count * frames * height * columns
    grad_block = jnp.stack(block_terms).reshape(3, 3, 3, channels, channels) * (total_cells ** -0.5)
    grad_down = jnp.stack(down_terms).reshape(3, 3, 3, channels, wide_channels) * ((total_cells / 8) ** -0.5)
    return latents.astype(jnp.bfloat16), grad_video, grad_block, grad_down
```

```python
import functools

import jax
import jax.numpy as jnp
from jax import lax
from jax.experimental import pallas as pl
from jax.experimental.pallas import tpu as pltpu
from jax.sharding import PartitionSpec as P

BF = jnp.bfloat16
F32 = jnp.float32
MESH = pl.DeviceIdType.MESH
SPLIT = 41


def shifted(value, axis, steps):
    count = lax.axis_size(axis)
    pairs = [(i, i + steps) for i in range(count) if 0 <= i + steps < count]
    return lax.ppermute(value, axis, pairs)


def before(x):
    rolled = pltpu.roll(x, 1, axis=x.ndim - 2)
    index = lax.broadcasted_iota(jnp.int32, x.shape, x.ndim - 2)
    return jnp.where(index == 0, 0.0, rolled)


def after(x):
    size = x.shape[-2]
    rolled = pltpu.roll(x, size - 1, axis=x.ndim - 2)
    index = lax.broadcasted_iota(jnp.int32, x.shape, x.ndim - 2)
    return jnp.where(index == size - 1, 0.0, rolled)


def nn(x, y):
    return lax.dot_general(x, y, (((1,), (0,)), ((), ())), preferred_element_type=F32)


def nt(x, y):
    return lax.dot_general(x, y, (((1,), (1,)), ((), ())), preferred_element_type=F32)


def flat(x):
    return x.reshape(-1, x.shape[-1])


def put(g_ref, k, value):
    stream, at = (0, k) if k < SPLIT else (1, k - SPLIT)
    g_ref[stream, at * 8 : at * 8 + 8] = value.reshape(8, 16, 128)


def compute_kernel(v_ref, c_ref, bw_ref, dw_ref, lat_ref, gv_ref, g_ref, a4, s4, g4, c2, w4, bt, dt):
    c = 128
    inner = (lax.axis_index("rows") > 0).astype(F32)
    zero = jnp.zeros((c, c), BF)
    units = g_ref.shape[1]
    g_ref[0, SPLIT * 8 :] = jnp.zeros((units - SPLIT * 8, 16, 128), F32)
    g_ref[1, (81 - SPLIT) * 8 :] = jnp.zeros((units - (81 - SPLIT) * 8, 16, 128), F32)
    planes = [(a, b) for a in range(3) for b in range(3)]
    for k, (a, b) in enumerate(planes):
        w = [bw_ref[a, b, i] for i in range(3)]
        d = [dw_ref[a, b, i] for i in range(3)]
        for i in range(3):
            w4[k, i * c : i * c + c, 0:c] = w[i]
            w4[k, (i + 1) * c : (i + 2) * c, c:] = w[i]
            bt[k, 0:c, (2 - i) * c : (3 - i) * c] = w[i]
            bt[k, c:, (3 - i) * c : (4 - i) * c] = w[i]
        w4[k, 3 * c :, 0:c] = zero
        w4[k, 0:c, c:] = zero
        bt[k, 0:c, 3 * c :] = zero
        bt[k, c:, 0:c] = zero
        dt[k, 0:c, 0 : 2 * c] = d[1]
        dt[k, c:, 0 : 2 * c] = d[2]
        dt[k, c:, 2 * c :] = d[0]
        dt[k, 0:c, 2 * c :] = jnp.zeros((c, 2 * c), BF)
    for t in range(3):
        cot = c_ref[t]
        c2[t, :, :, 0 : 2 * c] = cot
        c2[t, :, :, 2 * c :] = after(cot.astype(F32)).astype(BF)
    frame_sets = {0: [(1, 0)], 1: [(0, 1), (2, 0)]}
    row_sets = {0: [(1, 1)], 1: [(0, 1), (2, 0)]}
    for fp in range(2):
        for rp in range(2):
            total = None
            for a, t in frame_sets[fp]:
                for b, i in row_sets[rp]:
                    term = nt(flat(c2[t : t + 2, i : i + 3]), dt[a * 3 + b])
                    total = term if total is None else total + term
            gs = total.astype(BF).reshape(2, 3, 64, 2 * c).astype(F32)
            low = before(gs[..., c:])
            high = after(gs[..., :c])
            for h in range(2):
                for r in range(3):
                    keep = inner if (rp == 1 and r == 0) else None
                    row = jnp.concatenate([low[h, r], gs[h, r], high[h, r]], axis=-1)
                    if keep is not None:
                        row = row * keep
                    g4[2 * h + fp, 2 * r + (1 - rp)] = row.astype(BF)
    for f in range(5):
        v = v_ref[f].astype(F32)
        act = (v / (1.0 + jnp.exp(-v))).astype(BF).astype(F32)
        a4[f, :, :, 0:c] = before(act[..., c:]).astype(BF)
        a4[f, :, :, c : 3 * c] = act.astype(BF)
        a4[f, :, :, 3 * c :] = after(act[..., :c]).astype(BF)
    own_t = flat(a4[3:5, 2:6, :, c : 3 * c]).astype(F32).T.astype(BF)
    grad_act = None
    for k, (a, b) in enumerate(planes):
        window = flat(g4[2 - a : 4 - a, 2 - b : 6 - b])
        term = nt(window, bt[k])
        grad_act = term if grad_act is None else grad_act + term
        outer = nn(own_t, window)
        even, odd = outer[:c], outer[c:]
        put(g_ref, k * 3 + 2, even[:, 0:c] + odd[:, c : 2 * c])
        put(g_ref, k * 3 + 1, even[:, c : 2 * c] + odd[:, 2 * c : 3 * c])
        put(g_ref, k * 3, even[:, 2 * c : 3 * c] + odd[:, 3 * c :])
    v = flat(v_ref[3:5, 2:6]).astype(F32)
    sig = 1.0 / (1.0 + jnp.exp(-v))
    own_g = flat(g4[0:2, 1:5, :, c : 3 * c]).astype(F32)
    gv = own_g + grad_act * sig * (1.0 + v * (1.0 - sig))
    gv_ref[...] = gv.astype(BF).reshape(2, 4, 64, 2 * c)
    branch = None
    for k, (a, b) in enumerate(planes):
        term = nn(flat(a4[a : a + 3, b : b + 5]), w4[k])
        branch = term if branch is None else branch + term
    branch = branch.reshape(3, 5, 64, 2 * c)
    for f in range(3):
        for r in range(5):
            row = (v_ref[f + 2, r + 1].astype(F32) + branch[f, r]).astype(BF).astype(F32)
            if r == 0:
                row = row * inner
            s4[f, r, :, 0:c] = before(row[:, c:]).astype(BF)
            s4[f, r, :, c:] = row.astype(BF)
    latents = None
    for a, b in planes:
        lhs = jnp.concatenate([s4[a, b], s4[a, b + 2]], axis=0)
        term = nn(lhs, dw_ref[a, b].reshape(3 * c, 2 * c))
        latents = term if latents is None else latents + term
    lat_ref[...] = latents.astype(BF).reshape(1, 2, 64, 2 * c)
    turned = {}
    for s in range(2):
        for p in range(2):
            pair = jnp.concatenate([s4[s + 1, p + 1, :, c:], s4[s + 1, p + 3, :, c:]], axis=0)
            turned[s, p] = pair.astype(F32).T.astype(BF)
    frame_map = [(1, 1), (0, 0), (1, 0)]
    row_map = [(1, 2), (0, 1), (1, 1)]
    for k, (a, b) in enumerate(planes):
        (s, t), (p, i) = frame_map[a], row_map[b]
        outer = nn(turned[s, p], flat(c2[t, i : i + 2]))
        parts = [outer[c:, 2 * c :], outer[:c, : 2 * c], outer[c:, : 2 * c]]
        for tap in range(3):
            at = 27 + (k * 3 + tap) * 2
            put(g_ref, at, parts[tap][:, :c])
            put(g_ref, at + 1, parts[tap][:, c:])


def stage_lists(rows, dp, tm):
    row_stage = ("rows", 1, rows)
    if dp == 4:
        return [
            [row_stage, ("dp", 1, 2), ("dp", 2, 2), ("tm", 1, tm)],
            [row_stage, ("dp", 2, 2), ("dp", 1, 2), ("tm", 1, tm)],
        ]
    return [[row_stage, ("dp", 1, dp), ("tm", 1, tm)]] * 2


def member(stage):
    axis, step, count = stage
    return lax.rem(lax.axis_index(axis) // step, count)


def peer(stage, ahead):
    axis, step, count = stage
    mine = member(stage)
    other = lax.rem(mine + ahead, count)
    return other, {axis: lax.axis_index(axis) + (other - mine) * step}


def reduce_kernel(lists, copies, scales, x_ref, out_ref, acc, send, recv, load_sem, send_sem, recv_sem):
    units = acc.shape[1]
    barrier = pltpu.get_barrier_semaphore()
    greeted = 0
    for stage in lists[0]:
        for ahead in range(1, stage[2]):
            _, device = peer(stage, ahead)
            pl.semaphore_signal(barrier, inc=1, device_id=device, device_id_type=MESH)
            greeted += 1
    load = pltpu.make_async_copy(x_ref, acc, load_sem)
    load.start()
    load.wait()
    pl.semaphore_wait(barrier, greeted)

    offsets = [0, 0]
    lengths = [units, units]
    history = [[], []]
    slots = [0, 0]
    sems = [0, 0]
    pending = []

    def chunks(length):
        step = max(k for k in range(1, 12) if length % k == 0)
        return length // step, step

    def start(s, k):
        stage = lists[s][k]
        count = stage[2]
        piece = lengths[s] // count
        started = []
        for ahead in range(1, count):
            other, device = peer(stage, ahead)
            base = offsets[s] + other * piece
            loops, step = chunks(piece)

            @pl.loop(0, loops)
            def _(n, base=base, step=step):
                at = pl.ds(base + n * step, step)
                send[s, at] = acc[s, at].astype(BF)

            slot = pl.ds(slots[s], piece)
            copy = pltpu.make_async_remote_copy(
                src_ref=send.at[s, pl.ds(base, piece)],
                dst_ref=recv.at[s, slot],
                send_sem=send_sem.at[s, sems[s]],
                recv_sem=recv_sem.at[s, sems[s]],
                device_id=device,
                device_id_type=MESH,
            )
            copy.start()
            started.append((copy, slots[s]))
            slots[s] += piece
            sems[s] += 1
        history[s].append((offsets[s], lengths[s]))
        offsets[s] = offsets[s] + member(stage) * piece
        lengths[s] = piece
        return started

    def finish(s, started):
        loops, step = chunks(lengths[s])
        base = offsets[s]
        for copy, slot in started:
            copy.wait_recv()
            pending.append(copy)

        @pl.loop(0, loops)
        def _(n):
            at = pl.ds(base + n * step, step)
            value = acc[s, at]
            for _, slot in started:
                value = value + recv[s, pl.ds(slot + n * step, step)].astype(F32)
            acc[s, at] = value

    def spread(s, k):
        stage = lists[s][k]
        started = []
        for ahead in range(1, stage[2]):
            _, device = peer(stage, ahead)
            at = pl.ds(offsets[s], lengths[s])
            copy = pltpu.make_async_remote_copy(
                src_ref=out_ref.at[s, at],
                dst_ref=out_ref.at[s, at],
                send_sem=send_sem.at[s, sems[s]],
                recv_sem=recv_sem.at[s, sems[s]],
                device_id=device,
                device_id_type=MESH,
            )
            copy.start()
            started.append(copy)
            sems[s] += 1
        offsets[s], lengths[s] = history[s][k]
        return started

    last = len(lists[0]) - 1
    flying = [start(s, 0) for s in range(2)]
    for k in range(last + 1):
        for s in range(2):
            finish(s, flying[s])
            if k < last:
                flying[s] = start(s, k + 1)
            else:
                tile = lax.broadcasted_iota(jnp.int32, (lengths[s], 16, 128), 0) + offsets[s]
                value = acc[s, pl.ds(offsets[s], lengths[s])]
                first = scales[0] if s == 0 else scales[1]
                scaled = value * jnp.where(tile < 27 * 8, first, scales[1])
                out_ref[s, pl.ds(offsets[s], lengths[s])] = scaled.astype(BF)
                flying[s] = spread(s, last)
    for k in range(last, -1, -1):
        for s in range(2):
            for copy in flying[s]:
                copy.wait_recv()
                pending.append(copy)
            if k > 0:
                flying[s] = spread(s, k - 1)
    for copy in pending:
        copy.wait_send()


def local(video_cells, block_weight, down_weight, cotangent):
    frames, height, columns, channels = video_cells.shape[1:]
    wide = down_weight.shape[-1]
    dp, rows, tm = (lax.axis_size(name) for name in ("dp", "rows", "tm"))
    devices = dp * rows * tm
    video = video_cells[0].reshape(frames, height, columns // 2, 2 * channels)
    cot = cotangent[0]
    video_x = jnp.concatenate([shifted(video[1:], "tm", 2), shifted(video, "tm", 1), video], axis=0)
    video_x = jnp.concatenate(
        [shifted(video_x[:, height - 2 :], "rows", 1), video_x, shifted(video_x[:, :1], "rows", -1)], axis=1
    )
    cot_x = jnp.concatenate([cot, shifted(cot, "tm", -1), shifted(cot, "tm", -2)], axis=0)
    cot_x = jnp.concatenate(
        [shifted(cot_x[:, 1:], "rows", 1), cot_x, shifted(cot_x[:, :1], "rows", -1)], axis=1
    )
    unit = -(-SPLIT * 8 // devices)
    units = unit * devices
    vmem = pl.BlockSpec(memory_space=pltpu.VMEM)
    latents, grad_video, terms = pl.pallas_call(
        compute_kernel,
        out_shape=(
            jax.ShapeDtypeStruct((1, 2, 64, 256), BF),
            jax.ShapeDtypeStruct((2, 4, 64, 256), BF),
            jax.ShapeDtypeStruct((2, units, 16, 128), F32),
        ),
        in_specs=[vmem] * 4,
        out_specs=(vmem,) * 3,
        scratch_shapes=[
            pltpu.VMEM((5, 7, 64, 512), BF),
            pltpu.VMEM((3, 5, 64, 384), BF),
            pltpu.VMEM((4, 6, 64, 512), BF),
            pltpu.VMEM((3, 4, 64, 512), BF),
            pltpu.VMEM((9, 512, 256), BF),
            pltpu.VMEM((9, 256, 512), BF),
            pltpu.VMEM((9, 256, 512), BF),
        ],
        compiler_params=pltpu.CompilerParams(vmem_limit_bytes=56 * 1024 * 1024),
        name="conv_parts",
    )(video_x, cot_x, block_weight, down_weight)
    lists = stage_lists(rows, dp, tm)
    copies = sum(stage[2] - 1 for stage in lists[0])
    slots, length = 0, units
    for stage in lists[0]:
        length //= stage[2]
        slots += (stage[2] - 1) * length
    cells = frames * height * columns * devices
    scales = (float(cells) ** -0.5, float(cells / 8) ** -0.5)
    summed = pl.pallas_call(
        functools.partial(reduce_kernel, lists, copies, scales),
        out_shape=jax.ShapeDtypeStruct((2, units, 16, 128), BF),
        in_specs=[pl.BlockSpec(memory_space=pl.ANY)],
        out_specs=vmem,
        scratch_shapes=[
            pltpu.VMEM((2, units, 16, 128), F32),
            pltpu.VMEM((2, units, 16, 128), BF),
            pltpu.VMEM((2, slots, 16, 128), BF),
            pltpu.SemaphoreType.DMA,
            pltpu.SemaphoreType.DMA((2, 2 * copies)),
            pltpu.SemaphoreType.DMA((2, 2 * copies)),
        ],
        compiler_params=pltpu.CompilerParams(
            collective_id=0, has_side_effects=True, vmem_limit_bytes=32 * 1024 * 1024
        ),
        name="sum_parts",
    )(terms)
    grad_block = summed[0, : 27 * 8].astype(F32).reshape(3, 3, 3, channels, channels)
    down = jnp.concatenate(
        [summed[0, 27 * 8 : SPLIT * 8], summed[1, : (81 - SPLIT) * 8]], axis=0
    ).reshape(3, 3, 3, 2, channels, wide // 2)
    grad_down = jnp.concatenate([down[:, :, :, 0], down[:, :, :, 1]], axis=-1).astype(F32)
    return (
        latents.reshape(1, frames // 2, height // 2, columns // 2, wide),
        grad_video.reshape(1, frames, height, columns, channels),
        grad_block,
        grad_down,
    )


def solution(mesh):
    return jax.shard_map(
        local,
        mesh=mesh,
        in_specs=(P("dp", "tm", "rows", None, None), P(), P(), P("dp", "tm", "rows", None, None)),
        out_specs=(P("dp", "tm", "rows", None, None), P("dp", "tm", "rows", None, None), P(), P()),
        check_vma=False,
    )
```

```python
import functools

import jax
import jax.numpy as jnp
from jax import lax
from jax.experimental import pallas as pl
from jax.experimental.pallas import tpu as pltpu
from jax.sharding import PartitionSpec as P

BF = jnp.bfloat16
F32 = jnp.float32
MESH = pl.DeviceIdType.MESH
SPLIT = 41


def shifted(value, axis, steps):
    count = lax.axis_size(axis)
    pairs = [(i, i + steps) for i in range(count) if 0 <= i + steps < count]
    return lax.ppermute(value, axis, pairs)


def before(x):
    rolled = pltpu.roll(x, 1, axis=x.ndim - 2)
    index = lax.broadcasted_iota(jnp.int32, x.shape, x.ndim - 2)
    return jnp.where(index == 0, 0.0, rolled)


def after(x):
    size = x.shape[-2]
    rolled = pltpu.roll(x, size - 1, axis=x.ndim - 2)
    index = lax.broadcasted_iota(jnp.int32, x.shape, x.ndim - 2)
    return jnp.where(index == size - 1, 0.0, rolled)


def nn(x, y):
    return lax.dot_general(x, y, (((1,), (0,)), ((), ())), preferred_element_type=F32)


def nt(x, y):
    return lax.dot_general(x, y, (((1,), (1,)), ((), ())), preferred_element_type=F32)


def flat(x):
    return x.reshape(-1, x.shape[-1])


def put(g_ref, k, value):
    stream, at = (0, k) if k < SPLIT else (1, k - SPLIT)
    g_ref[stream, at * 8 : at * 8 + 8] = value.reshape(8, 16, 128)


def compute_kernel(v_ref, c_ref, bw_ref, dw_ref, lat_ref, gv_ref, g_ref, a4, s4, g4, c2, w4, bt, dt):
    c = 128
    inner = (lax.axis_index("rows") > 0).astype(F32)
    zero = jnp.zeros((c, c), BF)
    units = g_ref.shape[1]
    g_ref[0, SPLIT * 8 :] = jnp.zeros((units - SPLIT * 8, 16, 128), F32)
    g_ref[1, (81 - SPLIT) * 8 :] = jnp.zeros((units - (81 - SPLIT) * 8, 16, 128), F32)
    planes = [(a, b) for a in range(3) for b in range(3)]
    for k, (a, b) in enumerate(planes):
        w = [bw_ref[a, b, i] for i in range(3)]
        d = [dw_ref[a, b, i] for i in range(3)]
        for i in range(3):
            w4[k, i * c : i * c + c, 0:c] = w[i]
            w4[k, (i + 1) * c : (i + 2) * c, c:] = w[i]
            bt[k, 0:c, (2 - i) * c : (3 - i) * c] = w[i]
            bt[k, c:, (3 - i) * c : (4 - i) * c] = w[i]
        w4[k, 3 * c :, 0:c] = zero
        w4[k, 0:c, c:] = zero
        bt[k, 0:c, 3 * c :] = zero
        bt[k, c:, 0:c] = zero
        dt[k, 0:c, 0 : 2 * c] = d[1]
        dt[k, c:, 0 : 2 * c] = d[2]
        dt[k, c:, 2 * c :] = d[0]
        dt[k, 0:c, 2 * c :] = jnp.zeros((c, 2 * c), BF)
    for t in range(3):
        cot = c_ref[t]
        c2[t, :, :, 0 : 2 * c] = cot
        c2[t, :, :, 2 * c :] = after(cot.astype(F32)).astype(BF)
    frame_sets = {0: [(1, 0)], 1: [(0, 1), (2, 0)]}
    row_sets = {0: [(1, 1)], 1: [(0, 1), (2, 0)]}
    for fp in range(2):
        for rp in range(2):
            total = None
            for a, t in frame_sets[fp]:
                for b, i in row_sets[rp]:
                    term = nt(flat(c2[t : t + 2, i : i + 3]), dt[a * 3 + b])
                    total = term if total is None else total + term
            gs = total.astype(BF).reshape(2, 3, 64, 2 * c).astype(F32)
            low = before(gs[..., c:])
            high = after(gs[..., :c])
            for h in range(2):
                for r in range(3):
                    keep = inner if (rp == 1 and r == 0) else None
                    row = jnp.concatenate([low[h, r], gs[h, r], high[h, r]], axis=-1)
                    if keep is not None:
                        row = row * keep
                    g4[2 * h + fp, 2 * r + (1 - rp)] = row.astype(BF)
    for f in range(5):
        v = v_ref[f].astype(F32)
        act = (v / (1.0 + jnp.exp(-v))).astype(BF).astype(F32)
        a4[f, :, :, 0:c] = before(act[..., c:]).astype(BF)
        a4[f, :, :, c : 3 * c] = act.astype(BF)
        a4[f, :, :, 3 * c :] = after(act[..., :c]).astype(BF)
    own_t = flat(a4[3:5, 2:6, :, c : 3 * c]).astype(F32).T.astype(BF)
    grad_act = None
    for k, (a, b) in enumerate(planes):
        window = flat(g4[2 - a : 4 - a, 2 - b : 6 - b])
        term = nt(window, bt[k])
        grad_act = term if grad_act is None else grad_act + term
        outer = nn(own_t, window)
        even, odd = outer[:c], outer[c:]
        put(g_ref, k * 3 + 2, even[:, 0:c] + odd[:, c : 2 * c])
        put(g_ref, k * 3 + 1, even[:, c : 2 * c] + odd[:, 2 * c : 3 * c])
        put(g_ref, k * 3, even[:, 2 * c : 3 * c] + odd[:, 3 * c :])
    v = flat(v_ref[3:5, 2:6]).astype(F32)
    sig = 1.0 / (1.0 + jnp.exp(-v))
    own_g = flat(g4[0:2, 1:5, :, c : 3 * c]).astype(F32)
    gv = own_g + grad_act * sig * (1.0 + v * (1.0 - sig))
    gv_ref[...] = gv.astype(BF).reshape(2, 4, 64, 2 * c)
    branch = None
    for k, (a, b) in enumerate(planes):
        term = nn(flat(a4[a : a + 3, b : b + 5]), w4[k])
        branch = term if branch is None else branch + term
    branch = branch.reshape(3, 5, 64, 2 * c)
    for f in range(3):
        for r in range(5):
            row = (v_ref[f + 2, r + 1].astype(F32) + branch[f, r]).astype(BF).astype(F32)
            if r == 0:
                row = row * inner
            s4[f, r, :, 0:c] = before(row[:, c:]).astype(BF)
            s4[f, r, :, c:] = row.astype(BF)
    latents = None
    for a, b in planes:
        lhs = jnp.concatenate([s4[a, b], s4[a, b + 2]], axis=0)
        term = nn(lhs, dw_ref[a, b].reshape(3 * c, 2 * c))
        latents = term if latents is None else latents + term
    lat_ref[...] = latents.astype(BF).reshape(1, 2, 64, 2 * c)
    turned = {}
    for s in range(2):
        for p in range(2):
            pair = jnp.concatenate([s4[s + 1, p + 1, :, c:], s4[s + 1, p + 3, :, c:]], axis=0)
            turned[s, p] = pair.astype(F32).T.astype(BF)
    frame_map = [(1, 1), (0, 0), (1, 0)]
    row_map = [(1, 2), (0, 1), (1, 1)]
    for k, (a, b) in enumerate(planes):
        (s, t), (p, i) = frame_map[a], row_map[b]
        outer = nn(turned[s, p], flat(c2[t, i : i + 2]))
        parts = [outer[c:, 2 * c :], outer[:c, : 2 * c], outer[c:, : 2 * c]]
        for tap in range(3):
            at = 27 + (k * 3 + tap) * 2
            put(g_ref, at, parts[tap][:, :c])
            put(g_ref, at + 1, parts[tap][:, c:])


def stage_lists(rows, dp, tm):
    row_stage = ("rows", 1, rows)
    if dp == 4:
        return [
            [row_stage, ("dp", 1, 2), ("dp", 2, 2), ("tm", 1, tm)],
            [row_stage, ("dp", 2, 2), ("dp", 1, 2), ("tm", 1, tm)],
        ]
    return [[row_stage, ("dp", 1, dp), ("tm", 1, tm)]] * 2


def member(stage):
    axis, step, count = stage
    return lax.rem(lax.axis_index(axis) // step, count)


def peer(stage, ahead):
    axis, step, count = stage
    mine = member(stage)
    other = lax.rem(mine + ahead, count)
    return other, {axis: lax.axis_index(axis) + (other - mine) * step}


def reduce_kernel(lists, copies, scales, x_ref, out_ref, acc, send, recv, send_sem, recv_sem):
    units = acc.shape[1]
    barrier = pltpu.get_barrier_semaphore()
    greeted = 0
    for stage in lists[0]:
        for ahead in range(1, stage[2]):
            _, device = peer(stage, ahead)
            pl.semaphore_signal(barrier, inc=1, device_id=device, device_id_type=MESH)
            greeted += 1
    pl.semaphore_wait(barrier, greeted)

    offsets = [0, 0]
    lengths = [units, units]
    history = [[], []]
    slots = [0, 0]
    sems = [0, 0]
    pending = []

    def chunks(length):
        step = max(k for k in range(1, 12) if length % k == 0)
        return length // step, step

    def start(s, k):
        stage = lists[s][k]
        source = x_ref if k == 0 else acc
        count = stage[2]
        piece = lengths[s] // count
        started = []
        for ahead in range(1, count):
            other, device = peer(stage, ahead)
            base = offsets[s] + other * piece
            loops, step = chunks(piece)

            @pl.loop(0, loops)
            def _(n, base=base, step=step):
                at = pl.ds(base + n * step, step)
                send[s, at] = source[s, at].astype(BF)

            slot = pl.ds(slots[s], piece)
            copy = pltpu.make_async_remote_copy(
                src_ref=send.at[s, pl.ds(base, piece)],
                dst_ref=recv.at[s, slot],
                send_sem=send_sem.at[s, sems[s]],
                recv_sem=recv_sem.at[s, sems[s]],
                device_id=device,
                device_id_type=MESH,
            )
            copy.start()
            started.append((copy, slots[s]))
            slots[s] += piece
            sems[s] += 1
        history[s].append((offsets[s], lengths[s]))
        offsets[s] = offsets[s] + member(stage) * piece
        lengths[s] = piece
        return started

    def finish(s, k, started):
        source = x_ref if k == 0 else acc
        loops, step = chunks(lengths[s])
        base = offsets[s]
        for copy, slot in started:
            copy.wait_recv()
            pending.append(copy)

        @pl.loop(0, loops)
        def _(n):
            at = pl.ds(base + n * step, step)
            value = source[s, at]
            for _, slot in started:
                value = value + recv[s, pl.ds(slot + n * step, step)].astype(F32)
            acc[s, at] = value

    def spread(s, k):
        stage = lists[s][k]
        started = []
        for ahead in range(1, stage[2]):
            _, device = peer(stage, ahead)
            at = pl.ds(offsets[s], lengths[s])
            copy = pltpu.make_async_remote_copy(
                src_ref=out_ref.at[s, at],
                dst_ref=out_ref.at[s, at],
                send_sem=send_sem.at[s, sems[s]],
                recv_sem=recv_sem.at[s, sems[s]],
                device_id=device,
                device_id_type=MESH,
            )
            copy.start()
            started.append(copy)
            sems[s] += 1
        offsets[s], lengths[s] = history[s][k]
        return started

    last = len(lists[0]) - 1
    flying = [start(s, 0) for s in range(2)]
    for k in range(last + 1):
        for s in range(2):
            finish(s, k, flying[s])
            if k < last:
                flying[s] = start(s, k + 1)
            else:
                tile = lax.broadcasted_iota(jnp.int32, (lengths[s], 16, 128), 0) + offsets[s]
                value = acc[s, pl.ds(offsets[s], lengths[s])]
                first = scales[0] if s == 0 else scales[1]
                scaled = value * jnp.where(tile < 27 * 8, first, scales[1])
                out_ref[s, pl.ds(offsets[s], lengths[s])] = scaled.astype(BF)
                flying[s] = spread(s, last)
    for k in range(last, -1, -1):
        for s in range(2):
            for copy in flying[s]:
                copy.wait_recv()
                pending.append(copy)
            if k > 0:
                flying[s] = spread(s, k - 1)
    for copy in pending:
        copy.wait_send()


def local(video_cells, block_weight, down_weight, cotangent):
    frames, height, columns, channels = video_cells.shape[1:]
    wide = down_weight.shape[-1]
    dp, rows, tm = (lax.axis_size(name) for name in ("dp", "rows", "tm"))
    devices = dp * rows * tm
    video = video_cells[0].reshape(frames, height, columns // 2, 2 * channels)
    cot = cotangent[0]
    video_x = jnp.concatenate([shifted(video[1:], "tm", 2), shifted(video, "tm", 1), video], axis=0)
    video_x = jnp.concatenate(
        [shifted(video_x[:, height - 2 :], "rows", 1), video_x, shifted(video_x[:, :1], "rows", -1)], axis=1
    )
    cot_x = jnp.concatenate([cot, shifted(cot, "tm", -1), shifted(cot, "tm", -2)], axis=0)
    cot_x = jnp.concatenate(
        [shifted(cot_x[:, 1:], "rows", 1), cot_x, shifted(cot_x[:, :1], "rows", -1)], axis=1
    )
    unit = -(-SPLIT * 8 // devices)
    units = unit * devices
    vmem = pl.BlockSpec(memory_space=pltpu.VMEM)
    latents, grad_video, terms = pl.pallas_call(
        compute_kernel,
        out_shape=(
            jax.ShapeDtypeStruct((1, 2, 64, 256), BF),
            jax.ShapeDtypeStruct((2, 4, 64, 256), BF),
            jax.ShapeDtypeStruct((2, units, 16, 128), F32),
        ),
        in_specs=[vmem] * 4,
        out_specs=(vmem,) * 3,
        scratch_shapes=[
            pltpu.VMEM((5, 7, 64, 512), BF),
            pltpu.VMEM((3, 5, 64, 384), BF),
            pltpu.VMEM((4, 6, 64, 512), BF),
            pltpu.VMEM((3, 4, 64, 512), BF),
            pltpu.VMEM((9, 512, 256), BF),
            pltpu.VMEM((9, 256, 512), BF),
            pltpu.VMEM((9, 256, 512), BF),
        ],
        compiler_params=pltpu.CompilerParams(vmem_limit_bytes=32 * 1024 * 1024),
        name="conv_parts",
    )(video_x, cot_x, block_weight, down_weight)
    lists = stage_lists(rows, dp, tm)
    copies = sum(stage[2] - 1 for stage in lists[0])
    slots, length = 0, units
    for stage in lists[0]:
        length //= stage[2]
        slots += (stage[2] - 1) * length
    cells = frames * height * columns * devices
    scales = (float(cells) ** -0.5, float(cells / 8) ** -0.5)
    summed = pl.pallas_call(
        functools.partial(reduce_kernel, lists, copies, scales),
        out_shape=jax.ShapeDtypeStruct((2, units, 16, 128), BF),
        in_specs=[vmem],
        out_specs=vmem,
        scratch_shapes=[
            pltpu.VMEM((2, units, 16, 128), F32),
            pltpu.VMEM((2, units, 16, 128), BF),
            pltpu.VMEM((2, slots, 16, 128), BF),
            pltpu.SemaphoreType.DMA((2, 2 * copies)),
            pltpu.SemaphoreType.DMA((2, 2 * copies)),
        ],
        compiler_params=pltpu.CompilerParams(
            collective_id=0, has_side_effects=True, vmem_limit_bytes=32 * 1024 * 1024
        ),
        name="sum_parts",
    )(terms)
    grad_block = summed[0, : 27 * 8].astype(F32).reshape(3, 3, 3, channels, channels)
    down = jnp.concatenate(
        [summed[0, 27 * 8 : SPLIT * 8], summed[1, : (81 - SPLIT) * 8]], axis=0
    ).reshape(3, 3, 3, 2, channels, wide // 2)
    grad_down = jnp.concatenate([down[:, :, :, 0], down[:, :, :, 1]], axis=-1).astype(F32)
    return (
        latents.reshape(1, frames // 2, height // 2, columns // 2, wide),
        grad_video.reshape(1, frames, height, columns, channels),
        grad_block,
        grad_down,
    )


def solution(mesh):
    return jax.shard_map(
        local,
        mesh=mesh,
        in_specs=(P("dp", "tm", "rows", None, None), P(), P(), P("dp", "tm", "rows", None, None)),
        out_specs=(P("dp", "tm", "rows", None, None), P("dp", "tm", "rows", None, None), P(), P()),
        check_vma=False,
    )
```
